32 devices in a mesh: wide: 8 (over z, y), narrow: 4 (over x, core).
Axes of the slice: x: 2, y: 2, z: 4, core: 2. Of those that a mesh axis runs over, the one named last changes fastest.
Arguments:
- old_fields: float32 [2048, 6, 16, 256], P(('wide', 'narrow')), may hold values from -6 to 6
- old_target: int32 [2048], P(('wide', 'narrow')), may hold values from 0 to 2047, as said below
- cut_flag: int32 [16, 8, 16], P('wide', 'narrow'), may hold values 0 or 1
- apertures: float32 [3, 256, 128, 256], P(None, 'wide', 'narrow'), may hold values from 0.2 to 1
- volume: float32 [256, 128, 256], P('wide', 'narrow'), may hold values from 0.5 to 1
- velocity: float32 [3, 256, 128, 256], P(None, 'wide', 'narrow'), may hold values from -4 to 4
- diffusivity: float32 [6], replicated, may hold values from 0.02 to 0.08
- coupling: float32 [6, 6], replicated, may hold values from -2.5 to 2.5
Outputs:
- adjoint_out: float32 [6, 256, 128, 256], P(None, 'wide', 'narrow')
The draws below stay inside these ranges and needn't reach their ends.
Inputs may be any that keep to these rules, and one draw needn't show every extreme that they name: `old_target`: every new block is named by exactly one old block. The blocks held by one device go only to devices with the same narrow index, exactly 8 to each device of that wide row, itself included. A block's number is (bx * 8 + by) * 16 + bz and its new owner is the device with wide index bx / 2 and narrow index by / 2, rounded down.
All inputs are finite; a program needn't handle non-finite values. No bound on the sum of `cut_flag` on one device may be relied on, other than what follows from the above.
Results may differ from the reference program's by a relative error of at most 0.00012.
Values sent between devices are 32-bit elements; how exact they have to be, the bound alone decides.
No kernel may reach another device: no remote copies, remote signals or barrier semaphores. Data moves between devices by JAX's collectives and lax.ppermute only.
A program may use at most 320 MiB of HBM per device.

```python
import math
import jax
import jax.numpy as jnp
from jax import lax

COMP = 6
BE = 16
BPX = 2
BPY = 2
BPZ = 16
BLK_DEV = 64
TOTAL_BLOCKS = 2048
GBX = 16
GBY = 8
GBZ = 16
NX = 256
NY = 128
NZ = 256


def draw_old_target(key, part):
    k_new, k_old = jax.random.split(jax.random.fold_in(key, 7))
    wide_count = GBX // BPX
    narrow_count = GBY // BPY
    per_peer = BLK_DEV // wide_count
    pairs = wide_count * narrow_count
    new_perm = jax.vmap(lambda one_key: jax.random.permutation(one_key, BLK_DEV))(jax.random.split(k_new, pairs)).reshape(wide_count, narrow_count, BLK_DEV)
    old_perm = jax.vmap(lambda one_key: jax.random.permutation(one_key, BLK_DEV))(jax.random.split(k_old, pairs)).reshape(wide_count, narrow_count, BLK_DEV)
    wide_new = jnp.arange(wide_count, dtype=jnp.int32)[:, None, None]
    narrow_index = jnp.arange(narrow_count, dtype=jnp.int32)[None, :, None]
    position = jnp.arange(BLK_DEV, dtype=jnp.int32)[None, None, :]
    new_slot = new_perm.astype(jnp.int32)
    block_x = wide_new * BPX + new_slot // (BPY * BPZ)
    block_y = narrow_index * BPY + new_slot // BPZ % BPY
    block_z = new_slot % BPZ
    target_ids = (block_x * GBY + block_y) * GBZ + block_z
    source_wide = position % wide_count
    source_rank = wide_new * per_peer + position // wide_count
    old_slot = old_perm.astype(jnp.int32)[source_wide, narrow_index, source_rank]
    flat_index = (source_wide * narrow_count + narrow_index) * BLK_DEV + old_slot
    target_ids = jnp.broadcast_to(target_ids, flat_index.shape)
    return jnp.zeros((TOTAL_BLOCKS,), jnp.int32).at[flat_index.reshape(-1)].set(target_ids.reshape(-1))


def plant(array, key, least, largest):
    longest = array.shape.index(max(array.shape))
    spots = []
    for shift in (0, 1):
        where = [jax.random.randint(jax.random.fold_in(key, axis), (), 0, length) for axis, length in enumerate(array.shape)]
        where[longest] = (where[longest] + shift) % array.shape[longest]
        spots.append(tuple(where))
    return array.at[spots[0]].set(least).at[spots[1]].set(largest)


def shard_levels(key, dims, cuts, low, top_value):
    gain, own = 1.0, jax.random.fold_in(key, 6)
    for dim, shards_of in cuts:
        draws = jnp.exp(jax.random.uniform(jax.random.fold_in(own, dim), (shards_of,), jnp.float32, low / len(cuts), top_value / len(cuts)))
        gain = gain * jnp.repeat(draws, dims[dim] // shards_of).reshape([-1 if axis == dim else 1 for axis in range(len(dims))])
    return gain


def centred(stream_key, dims, width, bound, cuts=(), kind=jnp.bfloat16):
    factor_of = shard_levels(stream_key, dims, cuts, -0.22, 0.18) if cuts else 1.0
    array = jax.random.normal(stream_key, dims, jnp.float32) * width * factor_of
    return jnp.minimum(jnp.maximum(array, -bound), bound).astype(kind)


def setup_inputs(seed: int = 0) -> dict:
    key_list = jax.random.split(jax.random.key(seed), 9)
    return {
        "old_fields": centred(key_list[0], (TOTAL_BLOCKS, COMP, BE, BE * BE), 1.0, 6.0, ((0, 32),), jnp.float32),
        "old_target": draw_old_target(jax.random.fold_in(key_list[8], 71), 0),
        "cut_flag": plant((jax.random.randint(key_list[2], (GBX, GBY, GBZ), 0, 3) < 1).astype(jnp.int32), jax.random.fold_in(key_list[2], 1), 0, 1),
        "apertures": jnp.clip(0.2 + 0.8 * jax.random.uniform(key_list[3], (3, NX, NY, NZ), jnp.float32) ** shard_levels(key_list[3], (3, NX, NY, NZ), ((1, 8), (2, 4)), -0.2, 0.2), 0.2, 1.0),
        "volume": jnp.clip(0.5 + 0.5 * jax.random.uniform(key_list[4], (NX, NY, NZ), jnp.float32) ** shard_levels(key_list[4], (NX, NY, NZ), ((0, 8), (1, 4)), -0.2, 0.2), 0.5, 1.0),
        "velocity": centred(key_list[5], (3, NX, NY, NZ), 1.0, 4.0, ((1, 8), (2, 4)), jnp.float32),
        "diffusivity": jnp.clip(jnp.exp(jax.random.uniform(key_list[6], (COMP,), jnp.float32, math.log(0.02), math.log(0.08))), 0.02, 0.08),
        "coupling": centred(key_list[7], (COMP, COMP), COMP ** -0.5, 2.5, (), jnp.float32),
    }


ADVECT = 0.2


def diffuse(padded, open_x, open_y, open_z):
    center = padded[:, 1:-1, 1:-1, :]
    line_x = padded[:, :, 1:-1, :]
    flux_x = open_x[None] * (line_x[:, 1:] - line_x[:, :-1])
    line_y = padded[:, 1:-1, :, :]
    flux_y = open_y[None] * (line_y[:, :, 1:] - line_y[:, :, :-1])
    line_z = jnp.pad(center, ((0, 0), (0, 0), (0, 0), (1, 1)))
    low_z = jnp.pad(open_z, ((0, 0), (0, 0), (1, 0)))
    flux_z = low_z[None] * (line_z[..., 1:] - line_z[..., :-1])
    return (flux_x[:, 1:] - flux_x[:, :-1]) + (flux_y[:, :, 1:] - flux_y[:, :, :-1]) + (flux_z[..., 1:] - flux_z[..., :-1])


def advect(padded, carry_x, carry_y, carry_z):
    center = padded[:, 1:-1, 1:-1, :]
    line_x = padded[:, :, 1:-1, :]
    flux_x = carry_x[None] * (line_x[:, 1:] + line_x[:, :-1]) * 0.5
    line_y = padded[:, 1:-1, :, :]
    flux_y = carry_y[None] * (line_y[:, :, 1:] + line_y[:, :, :-1]) * 0.5
    line_z = jnp.pad(center, ((0, 0), (0, 0), (0, 0), (1, 1)))
    low_z = jnp.pad(carry_z, ((0, 0), (0, 0), (1, 0)))
    flux_z = low_z[None] * (line_z[..., 1:] + line_z[..., :-1]) * 0.5
    return (flux_x[:, 1:] - flux_x[:, :-1]) + (flux_y[:, :, 1:] - flux_y[:, :, :-1]) + (flux_z[..., 1:] - flux_z[..., :-1])


def first_section(padded, geometry, viscous_rate, coupling):
    center = padded[:, 1:-1, 1:-1, :]
    return center + viscous_rate * diffuse(padded, geometry[0], geometry[1], geometry[2]) / geometry[6]


def second_section(padded, geometry, viscous_rate, coupling):
    center = padded[:, 1:-1, 1:-1, :]
    return center - ADVECT * advect(padded, geometry[3], geometry[4], geometry[5]) / geometry[6]


def third_section(padded, geometry, viscous_rate, coupling):
    center = padded[:, 1:-1, 1:-1, :]
    mixed = jnp.einsum("cj,jxyz->cxyz", coupling, center, precision=lax.Precision.HIGHEST)
    return center + viscous_rate * diffuse(padded, geometry[0], geometry[1], geometry[2]) / geometry[6] + mixed


def pad_sides(values):
    return jnp.pad(values, ((0, 0), (1, 1), (1, 1), (0, 0)))


def reference(old_fields, old_target, cut_flag, apertures, volume, velocity, diffusivity, coupling):
    relocated = jnp.zeros_like(old_fields).at[old_target].set(old_fields)
    adjoint = relocated.reshape(GBX, GBY, GBZ, COMP, BE, BE, BE).transpose(3, 0, 4, 1, 5, 2, 6).reshape(COMP, NX, NY, NZ)
    cut_cells = jnp.repeat(jnp.repeat(jnp.repeat(cut_flag, BE, 0), BE, 1), BE, 2) > 0
    face_open = jnp.where(cut_cells[None], apertures, 1.0)
    volume_fill = jnp.where(cut_cells, volume, 1.0)
    transport = face_open * velocity
    open_x = jnp.pad(face_open[0], ((1, 0), (0, 0), (0, 0)))
    open_y = jnp.pad(face_open[1], ((0, 0), (1, 0), (0, 0)))
    carry_x = jnp.pad(transport[0], ((1, 0), (0, 0), (0, 0)))
    carry_y = jnp.pad(transport[1], ((0, 0), (1, 0), (0, 0)))
    geometry = (open_x, open_y, face_open[2], carry_x, carry_y, transport[2], volume_fill)
    viscous_rate = diffusivity[:, None, None, None]
    after_one = first_section(pad_sides(adjoint), geometry, viscous_rate, coupling)
    after_two = second_section(pad_sides(after_one), geometry, viscous_rate, coupling)
    return third_section(pad_sides(after_two), geometry, viscous_rate, coupling)
```

```python
import functools

import jax
import jax.numpy as jnp
from jax import lax
from jax.experimental import pallas as pl
from jax.experimental.pallas import tpu as pltpu
from jax.sharding import PartitionSpec as P

BE = 16
BPX = 2
BPY = 2
BPZ = 16
COMP = 6
ADVECT = 0.2
W = 3
LX = BPX * BE
LY = BPY * BE
LZ = BPZ * BE
PX = LX + 2 * W
PY = LY + 8
CHUNKS = ((0, 3), (3, 3))
ANY = pl.BlockSpec(memory_space=pl.ANY)
SMEM = pl.BlockSpec(memory_space=pltpu.SMEM)
VMEM_LIMIT = 60 * 1024 * 1024


def pack_kernel(first, count, wide, layer, tgt, fields, out, ids, buf, tally, sem_in, sem_out):
    blocks = tgt.shape[0]
    per_peer = blocks // wide

    @pl.loop(0, wide)
    def _(d):
        tally[d] = 0

    @pl.loop(0, blocks)
    def _(b):
        t = tgt[b]
        bx = t // layer
        rest = t - bx * layer
        by = rest // BPZ
        bz = rest - by * BPZ
        dest = bx // BPX
        rank = tally[dest]
        tally[dest] = rank + 1
        place = dest * per_peer + rank
        ids[place] = ((bx - dest * BPX) * BPY + by % BPY) * BPZ + bz
        pltpu.make_async_copy(fields.at[b, pl.ds(first, count)], buf.at[place], sem_in).start()

    pltpu.make_async_copy(out, buf, sem_in).wait()
    copy = pltpu.make_async_copy(buf, out, sem_out)
    copy.start()
    copy.wait()


def pack(old_target, old_fields, first, count, wide, layer):
    blocks = old_fields.shape[0]
    shape = (blocks, count, BE, BE * BE)
    return pl.pallas_call(
        functools.partial(pack_kernel, first, count, wide, layer),
        out_shape=(
            jax.ShapeDtypeStruct(shape, jnp.float32),
            jax.ShapeDtypeStruct((blocks,), jnp.int32),
        ),
        in_specs=[SMEM, ANY],
        out_specs=(ANY, SMEM),
        scratch_shapes=[
            pltpu.VMEM(shape, jnp.float32),
            pltpu.SMEM((wide,), jnp.int32),
            pltpu.SemaphoreType.DMA,
            pltpu.SemaphoreType.DMA,
        ],
        compiler_params=pltpu.CompilerParams(vmem_limit_bytes=VMEM_LIMIT),
        cost_estimate=pl.CostEstimate(flops=0, bytes_accessed=8 * count * 16 * 256 * 64, transcendentals=0),
        name=f"pack{first}",
    )(old_target, old_fields)


def swap_groups(x):
    row = lax.broadcasted_iota(jnp.int32, x.shape, 0)
    group = lax.broadcasted_iota(jnp.int32, x.shape, 1) // BE

    def skew(x):
        for bit in (1, 2, 4):
            x = jnp.where((row & bit) != 0, pltpu.roll(x, 128 - BE * bit, 1), x)
        return x

    x = skew(x)
    for bit in (1, 2, 4):
        x = jnp.where((group & bit) != 0, pltpu.roll(x, bit, 0), x)
    return skew(x)


def unpack_kernel(count, ids, recv, v, face_lo, face_hi, stage, out, sem_in, sem_out):
    blocks = recv.shape[0]
    rows = count * BE

    @pl.loop(0, blocks)
    def _(b):
        slot = ids[b]
        bz = slot % BPZ
        place = slot - bz + (bz // 8) * 8 + (8 - bz % 8) % 8
        for half in range(2):
            pltpu.make_async_copy(
                recv.at[b, :, pl.ds(half * 128, 128)],
                stage.at[half, pl.ds(place * rows, rows)],
                sem_in,
            ).start()

    pltpu.make_async_copy(stage, stage, sem_in).wait()
    for bx in range(BPX):
        for by in range(BPY):
            base = (bx * BPY + by) * BPZ * rows

            @pl.loop(0, BE)
            def _(i):
                for c in range(count):
                    for half in range(2):
                        for top in range(2):
                            start = base + c * BE + i + top * 8 * rows
                            x = stage[half, pl.ds(start, 8, stride=rows), :]
                            out[
                                c, bx * BE + i, pl.ds(by * BE + half * 8, 8), pl.ds(top * 128, 128)
                            ] = swap_groups(x)

    copies = [
        pltpu.make_async_copy(out, v, sem_out.at[0]),
        pltpu.make_async_copy(out.at[:, pl.ds(0, W)], face_lo, sem_out.at[1]),
        pltpu.make_async_copy(out.at[:, pl.ds(LX - W, W)], face_hi, sem_out.at[2]),
    ]
    for copy in copies:
        copy.start()
    for copy in copies:
        copy.wait()


def unpack(ids, recv):
    blocks, count = recv.shape[:2]
    rows = count * BE
    face = jax.ShapeDtypeStruct((count, W, LY, LZ), jnp.float32)
    return pl.pallas_call(
        functools.partial(unpack_kernel, count),
        out_shape=(jax.ShapeDtypeStruct((count, LX, LY, LZ), jnp.float32), face, face),
        in_specs=[SMEM, ANY],
        out_specs=(ANY, ANY, ANY),
        scratch_shapes=[
            pltpu.VMEM((2, blocks * rows, 128), jnp.float32),
            pltpu.VMEM((count, LX, LY, LZ), jnp.float32),
            pltpu.SemaphoreType.DMA,
            pltpu.SemaphoreType.DMA((3,)),
        ],
        compiler_params=pltpu.CompilerParams(vmem_limit_bytes=VMEM_LIMIT),
        cost_estimate=pl.CostEstimate(flops=0, bytes_accessed=20 * count * LX * LY * LZ, transcendentals=0),
        name="unpack",
    )(ids, recv.reshape(blocks, rows, BE * BE))


def sections_kernel(first, count, has_prior, visc, coup, v, xlo, xhi, ylo, yhi, geo, *refs):
    if has_prior:
        prior, out, vb, a1, gb, tlo, thi, rb, sems = refs
    else:
        out, vb, a1, gb, tlo, thi, rb, sems = refs
    loads = [
        pltpu.make_async_copy(v, vb.at[:, pl.ds(W, LX), pl.ds(0, LY)], sems.at[0]),
        pltpu.make_async_copy(xlo, vb.at[:, pl.ds(0, W), pl.ds(0, LY)], sems.at[1]),
        pltpu.make_async_copy(xhi, vb.at[:, pl.ds(W + LX, W), pl.ds(0, LY)], sems.at[2]),
        pltpu.make_async_copy(ylo, tlo, sems.at[3]),
        pltpu.make_async_copy(yhi, thi, sems.at[4]),
        pltpu.make_async_copy(geo, gb, sems.at[5]),
    ]
    if has_prior:
        loads.append(pltpu.make_async_copy(prior, rb, sems.at[6]))
    for copy in loads:
        copy.start()
    for copy in loads:
        copy.wait()

    lane = lax.broadcasted_iota(jnp.int32, (PY, LZ), 1)
    top, bottom = lane == LZ - 1, lane == 0
    sub = lax.broadcasted_iota(jnp.int32, (8, LZ), 0)

    @pl.loop(0, PX)
    def _(x):
        for f in range(count):
            vb[f, x, pl.ds(LY, 8)] = jnp.where(sub < 4, thi[f, x], tlo[f, x])

    def up_y(a):
        return pltpu.roll(a, PY - 1, 0)

    def down_y(a):
        return pltpu.roll(a, 1, 0)

    def up_z(a):
        return jnp.where(top, 0.0, pltpu.roll(a, LZ - 1, 1))

    def down_z(a):
        return jnp.where(bottom, 0.0, pltpu.roll(a, 1, 1))

    def diffuse(src, f, x):
        c = src[f, x]
        flux = gb[0, x] * (src[f, x + 1] - c) - gb[0, x - 1] * (c - src[f, x - 1])
        flux_y = gb[1, x] * (up_y(c) - c)
        flux_z = gb[2, x] * (up_z(c) - c)
        return c, flux + (flux_y - down_y(flux_y)) + (flux_z - down_z(flux_z))

    def advect(src, f, x):
        c = src[f, x]
        flux = gb[3, x] * (src[f, x + 1] + c) - gb[3, x - 1] * (c + src[f, x - 1])
        flux_y = gb[4, x] * (up_y(c) + c)
        flux_z = gb[5, x] * (up_z(c) + c)
        return c, flux + (flux_y - down_y(flux_y)) + (flux_z - down_z(flux_z))

    @pl.loop(1, PX - 1)
    def _(x):
        for f in range(count):
            c, d = diffuse(vb, f, x)
            a1[f, x] = c + visc[first + f] * (gb[6, x] * d)

    @pl.loop(2, PX - 2)
    def _(x):
        for f in range(count):
            c, d = advect(a1, f, x)
            vb[f, x] = c - gb[6, x] * d

    @pl.loop(W, W + LX)
    def _(x):
        two = []
        own = []
        for f in range(count):
            c, d = diffuse(vb, f, x)
            own.append((c + visc[first + f] * (gb[6, x] * d))[:LY])
            two.append(c[:LY])
        for c in range(COMP):
            total = rb[c, x - W] if has_prior else None
            if first <= c < first + count:
                total = own[c - first] if total is None else total + own[c - first]
            for f in range(count):
                term = coup[c, first + f] * two[f]
                total = term if total is None else total + term
            rb[c, x - W] = total

    store = pltpu.make_async_copy(rb, out, sems.at[7])
    store.start()
    store.wait()


def sections(first, count, visc, coup, v, halos, geo, prior):
    operands = [visc, coup, v, *halos, geo]
    if prior is not None:
        operands.append(prior)
    cells = LX * LY * LZ
    return pl.pallas_call(
        functools.partial(sections_kernel, first, count, prior is not None),
        out_shape=jax.ShapeDtypeStruct((COMP, LX, LY, LZ), jnp.float32),
        in_specs=[SMEM, SMEM] + [ANY] * (len(operands) - 2),
        out_specs=ANY,
        scratch_shapes=[
            pltpu.VMEM((count, PX, PY, LZ), jnp.float32),
            pltpu.VMEM((count, PX, PY, LZ), jnp.float32),
            pltpu.VMEM((7, PX, PY, LZ), jnp.float32),
            pltpu.VMEM((count, PX, 8, LZ), jnp.float32),
            pltpu.VMEM((count, PX, 8, LZ), jnp.float32),
            pltpu.VMEM((COMP, LX, LY, LZ), jnp.float32),
            pltpu.SemaphoreType.DMA((8,)),
        ],
        compiler_params=pltpu.CompilerParams(vmem_limit_bytes=VMEM_LIMIT),
        cost_estimate=pl.CostEstimate(
            flops=cells * count * 80, bytes_accessed=4 * cells * (count + 20), transcendentals=0
        ),
        name=f"sections{first}",
    )(*operands)


def forward(value, axis):
    count = lax.axis_size(axis)
    return lax.ppermute(value, axis, [(i, i + 1) for i in range(count - 1)])


def backward(value, axis):
    count = lax.axis_size(axis)
    return lax.ppermute(value, axis, [(i + 1, i) for i in range(count - 1)])


def y_halos(xlo, center, xhi):
    rows = jnp.concatenate([a[:, :, LY - 8 :] for a in (xlo, center, xhi)], 1)
    low = forward(rows, "narrow")
    rows = jnp.concatenate([a[:, :, :8] for a in (xlo, center, xhi)], 1)
    return low, backward(rows, "narrow")


BELOW = ((0, 3), (0, 2), (0, 1), (1, 2), (1, 1), (2, 2), (2, 1), (6, 2), (6, 1), (3, 2), (3, 1), (4, 1), (5, 1))
ABOVE = ((0, 1), (0, 2), (1, 1), (1, 2), (2, 1), (2, 2), (6, 1), (6, 2), (3, 1), (4, 1), (5, 1))


def geometry(cut_flag, apertures, volume, velocity):
    cut_cells = jnp.repeat(jnp.repeat(jnp.repeat(cut_flag, BE, 0), BE, 1), BE, 2) > 0
    face_open = jnp.where(cut_cells[None], apertures, 1.0)
    inverse = 1.0 / jnp.where(cut_cells, volume, 1.0)
    transport = face_open * velocity * (0.5 * ADVECT)
    center = jnp.concatenate([face_open, transport, inverse[None]], 0)
    low = forward(jnp.stack([center[a, LX - d] for a, d in BELOW]), "wide")
    high = backward(jnp.stack([center[a, d - 1] for a, d in ABOVE]), "wide")
    zero = jnp.zeros((LY, LZ), jnp.float32)
    below = {key: low[n] for n, key in enumerate(BELOW)}
    above = {key: high[n] for n, key in enumerate(ABOVE)}
    xlo = jnp.stack([jnp.stack([below.get((a, d), zero) for d in (3, 2, 1)]) for a in range(7)])
    xhi = jnp.stack([jnp.stack([above.get((a, d), zero) for d in (1, 2, 3)]) for a in range(7)])
    ylo, yhi = y_halos(xlo, center, xhi)
    rows = jnp.concatenate([xlo, center, xhi], 1)
    edge = jnp.where(jnp.arange(8)[:, None] < 4, yhi, ylo)
    return jnp.concatenate([rows, edge], 2)


def on_device(old_fields, old_target, cut_flag, apertures, volume, velocity, diffusivity, coupling):
    wide = lax.axis_size("wide")
    layer = BPY * lax.axis_size("narrow") * BPZ
    received = []
    for first, count in CHUNKS:
        outgoing, ids = pack(old_target, old_fields, first, count, wide, layer)
        received.append(lax.all_to_all(outgoing, "wide", 0, 0, tiled=True))
        if first == 0:
            slots = lax.all_to_all(ids, "wide", 0, 0, tiled=True)
    geo = geometry(cut_flag, apertures, volume, velocity)
    result = None
    for (first, count), recv in zip(CHUNKS, received):
        v, face_lo, face_hi = unpack(slots, recv)
        xlo, xhi = forward(face_hi, "wide"), backward(face_lo, "wide")
        ylo, yhi = y_halos(xlo, v, xhi)
        result = sections(
            first, count, diffusivity, coupling, v, (xlo, xhi, ylo, yhi), geo, result
        )
    return result


def solution(mesh):
    in_specs = (
        P(("wide", "narrow"), None, None, None),
        P(("wide", "narrow")),
        P("wide", "narrow", None),
        P(None, "wide", "narrow", None),
        P("wide", "narrow", None),
        P(None, "wide", "narrow", None),
        P(),
        P(),
    )
    out_specs = P(None, "wide", "narrow", None)
    return jax.shard_map(
        on_device, mesh=mesh, in_specs=in_specs, out_specs=out_specs, check_vma=False
    )
```

```python
import functools

import jax
import jax.numpy as jnp
from jax import lax
from jax.experimental import pallas as pl
from jax.experimental.pallas import tpu as pltpu
from jax.sharding import PartitionSpec as P

BE = 16
BPX = 2
BPY = 2
BPZ = 16
COMP = 6
ADVECT = 0.2
W = 3
LX = BPX * BE
LY = BPY * BE
LZ = BPZ * BE
HZ = LZ // 2
PX = LX + 2 * W
PY = LY + 16
CHUNKS = ((0, 3), (3, 3))
ANY = pl.BlockSpec(memory_space=pl.ANY)
SMEM = pl.BlockSpec(memory_space=pltpu.SMEM)
VMEM_LIMIT = 60 * 1024 * 1024
PARTS = 4
UNROLL = 2
STRIP = 2

BELOW = ((0, 3), (0, 2), (0, 1), (1, 2), (1, 1), (2, 2), (2, 1), (6, 2), (6, 1), (3, 2), (3, 1), (4, 1), (5, 1))
ABOVE = ((0, 1), (0, 2), (1, 1), (1, 2), (2, 1), (2, 2), (6, 1), (6, 2), (3, 1), (4, 1), (5, 1))
CORNERS = (
    ((0, 1), (0, 2), (1, 1), (1, 2), (2, 1), (6, 1), (3, 1), (4, 1)),
    ((0, 1), (0, 2), (1, 1), (2, 1), (6, 1), (3, 1)),
    ((0, 1), (1, 1), (1, 2), (2, 1), (6, 1), (4, 1)),
    ((0, 1), (1, 1), (2, 1), (6, 1)),
)
STEPS = ((1, 1), (1, -1), (-1, 1), (-1, -1))


def struct(*shape):
    return jax.ShapeDtypeStruct(shape, jnp.float32)


def params():
    return pltpu.CompilerParams(vmem_limit_bytes=VMEM_LIMIT)


def cost(flops, moved):
    return pl.CostEstimate(flops=flops, bytes_accessed=moved, transcendentals=0)


def pack_kernel(first, count, wide, layer, tgt, fields, out, buf, header, ids, tally, sem_in, sem_out):
    blocks = tgt.shape[0]
    per_peer = blocks // wide
    rows = per_peer * count * BE

    @pl.loop(0, wide)
    def _(d):
        tally[d] = 0

    @pl.loop(0, blocks)
    def _(b):
        t = tgt[b]
        bx = t // layer
        rest = t - bx * layer
        by = rest // BPZ
        dest = bx // BPX
        rank = tally[dest]
        tally[dest] = rank + 1
        ids[dest * per_peer + rank] = ((bx - dest * BPX) * BPY + by % BPY) * BPZ + rest - by * BPZ
        pltpu.make_async_copy(
            fields.at[b, pl.ds(first, count)], buf.at[dest, rank], sem_in.at[dest]
        ).start()

    if first == 0:
        lane = lax.broadcasted_iota(jnp.int32, (8, HZ), 1)
        for dest in range(wide):
            places = jnp.zeros((8, HZ), jnp.int32)
            for rank in range(per_peer):
                places = jnp.where(lane == rank, ids[dest * per_peer + rank], places)
            header[dest] = places.astype(jnp.float32)
    copies = []
    for dest in range(wide):
        pltpu.make_async_copy(buf.at[dest], buf.at[dest], sem_in.at[dest]).wait()
        merged = buf.at[dest].reshape(rows, LZ)
        pairs = [
            (merged.at[:, pl.ds(half * HZ, HZ)], out.at[dest, half, pl.ds(0, rows)])
            for half in range(2)
        ]
        if first == 0:
            pairs.append((header.at[dest], out.at[dest, 0, pl.ds(rows, 8)]))
            pairs.append((header.at[dest], out.at[dest, 1, pl.ds(rows, 8)]))
        for n, (source, target) in enumerate(pairs):
            copies.append(pltpu.make_async_copy(source, target, sem_out.at[dest, n]))
            copies[-1].start()
    for copy in copies:
        copy.wait()


def pack(old_target, old_fields, first, count, wide, layer):
    blocks = old_fields.shape[0]
    per_peer = blocks // wide
    rows = per_peer * count * BE
    return pl.pallas_call(
        functools.partial(pack_kernel, first, count, wide, layer),
        out_shape=struct(wide, 2, rows + (8 if first == 0 else 0), HZ),
        in_specs=[SMEM, ANY],
        out_specs=ANY,
        scratch_shapes=[
            pltpu.VMEM((wide, per_peer, count, BE, LZ), jnp.float32),
            pltpu.VMEM((wide, 8, HZ), jnp.float32),
            pltpu.SMEM((blocks,), jnp.int32),
            pltpu.SMEM((wide,), jnp.int32),
            pltpu.SemaphoreType.DMA((wide,)),
            pltpu.SemaphoreType.DMA((wide, 4)),
        ],
        compiler_params=params(),
        cost_estimate=cost(0, 8 * wide * rows * LZ),
        name=f"pack{first}",
    )(old_target, old_fields)


def halo_copies(out, v, faces, sides, sems):
    pairs = [
        (out.at[:, :, :, pl.ds(0, 8)], sides[0]),
        (out.at[:, :, :, pl.ds(LY - 8, 8)], sides[1]),
        (out.at[:, :, pl.ds(0, W)], faces[0]),
        (out.at[:, :, pl.ds(LX - W, W)], faces[1]),
        (out, v),
    ]
    return [pltpu.make_async_copy(a, b, sems.at[n]) for n, (a, b) in enumerate(pairs)]


def swap_groups(x):
    row = lax.broadcasted_iota(jnp.int32, x.shape, 0)
    lane = lax.broadcasted_iota(jnp.int32, x.shape, 1)
    skew = (lane + BE * row) % HZ
    turn = (row - lane // BE) % 8
    x = jnp.take_along_axis(x, skew, axis=1, mode="promise_in_bounds")
    x = jnp.take_along_axis(x, turn, axis=0, mode="promise_in_bounds")
    return jnp.take_along_axis(x, skew, axis=1, mode="promise_in_bounds")


def unpack_kernel(count, ids, recv, *refs):
    v, face_lo, face_hi, side_lo, side_hi, stage, out, sem_in, sem_out = refs
    rows = count * BE
    wide = recv.shape[0]
    per_peer = ids.shape[0] // wide

    @pl.loop(0, wide)
    def _(step):
        for b in range(per_peer):
            slot = ids[step * per_peer + b]
            bz = slot % BPZ
            place = bz // 8 * 8 + (8 - bz % 8) % 8
            pltpu.make_async_copy(
                recv.at[step, :, pl.ds(b * rows, rows)],
                stage.at[:, slot // BPZ, :, place],
                sem_in.at[slot // BPZ],
            ).start()

    for q in range(BPX * BPY):
        pltpu.make_async_copy(stage.at[:, q], stage.at[:, q], sem_in.at[q]).wait()

        @pl.loop(0, BE, step=UNROLL)
        def _(i):
            for j in range(UNROLL):
                for c in range(count):
                    for half in range(2):
                        for top in range(2):
                            x = stage[half, q, c * BE + i + j, pl.ds(top * 8, 8), :]
                            row = q % BPY * BE + half * 8
                            out[c, top, q // BPY * BE + i + j, pl.ds(row, 8)] = swap_groups(x)

    copies = halo_copies(out, v, (face_lo, face_hi), (side_lo, side_hi), sem_out)
    for copy in copies:
        copy.start()
    for copy in copies:
        copy.wait()


def unpack(count, ids, recv):
    rows = count * BE
    face, side = struct(count, 2, W, LY, HZ), struct(count, 2, LX, 8, HZ)
    v, *edges = pl.pallas_call(
        functools.partial(unpack_kernel, count),
        out_shape=[struct(count, 2, LX, LY, HZ), face, face, side, side],
        in_specs=[SMEM, ANY],
        out_specs=[ANY] * 5,
        scratch_shapes=[
            pltpu.VMEM((2, BPX * BPY, rows, BPZ, HZ), jnp.float32),
            pltpu.VMEM((count, 2, LX, LY, HZ), jnp.float32),
            pltpu.SemaphoreType.DMA((BPX * BPY,)),
            pltpu.SemaphoreType.DMA((5,)),
        ],
        compiler_params=params(),
        cost_estimate=cost(0, 12 * count * LX * LY * LZ),
        name="unpack",
    )(ids, recv)
    return v, edges


def geometry_kernel(cut, apertures, volume, velocity, *refs):
    v, low, high, side_lo, side_hi, *corners = refs[:9]
    ap, vo, ve, mask, out, sem_in, sem_out, sem_layer = refs[9:]
    loads = [
        pltpu.make_async_copy(apertures, ap, sem_in.at[0]),
        pltpu.make_async_copy(volume, vo, sem_in.at[1]),
        pltpu.make_async_copy(velocity, ve, sem_in.at[2]),
    ]
    for copy in loads:
        copy.start()
    block_y = lax.broadcasted_iota(jnp.int32, (LY, LZ), 0) // BE
    block_z = lax.broadcasted_iota(jnp.int32, (LY, LZ), 1) // BE
    for bx in range(BPX):
        flags = jnp.zeros((LY, LZ), jnp.int32)
        for by in range(BPY):
            for bz in range(BPZ):
                flags = jnp.where((block_y == by) & (block_z == bz), cut[bx, by, bz], flags)
        mask[bx] = flags
    for copy in loads:
        copy.wait()
    for bx in range(BPX):

        @pl.loop(0, BE)
        def _(i):
            x = bx * BE + i
            for half in range(2):
                z = pl.ds(half * HZ, HZ)
                cut_here = mask[bx, :, z] > 0
                for d in range(3):
                    open_here = jnp.where(cut_here, ap[d, x, :, z], 1.0)
                    out[d, half, x] = open_here
                    out[3 + d, half, x] = open_here * ve[d, x, :, z] * (0.5 * ADVECT)
                out[6, half, x] = 1.0 / jnp.where(cut_here, vo[x, :, z], 1.0)

    copies = [
        pltpu.make_async_copy(out, v, sem_out.at[0]),
        pltpu.make_async_copy(out.at[:, :, :, pl.ds(0, 8)], side_lo, sem_out.at[1]),
        pltpu.make_async_copy(out.at[:, :, :, pl.ds(LY - 8, 8)], side_hi, sem_out.at[2]),
    ]
    n = 0
    for n, (a, d) in enumerate(BELOW):
        copies.append(pltpu.make_async_copy(out.at[a, :, LX - d], low.at[n], sem_layer.at[len(copies)]))
    for n, (a, d) in enumerate(ABOVE):
        copies.append(pltpu.make_async_copy(out.at[a, :, d - 1], high.at[n], sem_layer.at[len(copies)]))
    for (up, along), corner, layers in zip(STEPS, corners, CORNERS):
        y = pl.ds(LY - 8, 8) if along > 0 else pl.ds(0, 8)
        for n, (a, d) in enumerate(layers):
            x = LX - d if up > 0 else d - 1
            copies.append(
                pltpu.make_async_copy(out.at[a, :, x, y], corner.at[n], sem_layer.at[len(copies)])
            )
    for copy in copies:
        copy.start()
    for copy in copies:
        copy.wait()


def geometry(cut_flag, apertures, volume, velocity):
    side = struct(7, 2, LX, 8, HZ)
    low, high = struct(len(BELOW), 2, LY, HZ), struct(len(ABOVE), 2, LY, HZ)
    v, low, high, *rest = pl.pallas_call(
        geometry_kernel,
        out_shape=[struct(7, 2, LX, LY, HZ), low, high, side, side]
        + [struct(len(layers), 2, 8, HZ) for layers in CORNERS],
        in_specs=[SMEM, ANY, ANY, ANY],
        out_specs=[ANY] * 9,
        scratch_shapes=[
            pltpu.VMEM((3, LX, LY, LZ), jnp.float32),
            pltpu.VMEM((LX, LY, LZ), jnp.float32),
            pltpu.VMEM((3, LX, LY, LZ), jnp.float32),
            pltpu.VMEM((BPX, LY, LZ), jnp.int32),
            pltpu.VMEM((7, 2, LX, LY, HZ), jnp.float32),
            pltpu.SemaphoreType.DMA((3,)),
            pltpu.SemaphoreType.DMA((3,)),
            pltpu.SemaphoreType.DMA((64,)),
        ],
        compiler_params=params(),
        cost_estimate=cost(0, 64 * LX * LY * LZ),
        name="geometry",
    )(cut_flag, apertures, volume, velocity)
    return v, [high, low, *rest]


def shift(value, axis, by):
    count = lax.axis_size(axis)
    return lax.ppermute(value, axis, [(i, i + by) for i in range(count) if 0 <= i + by < count])


def shift_both(value, up, along):
    wide, narrow = lax.axis_size("wide"), lax.axis_size("narrow")
    pairs = [
        (w * narrow + n, (w + up) * narrow + n + along)
        for w in range(wide)
        for n in range(narrow)
        if 0 <= w + up < wide and 0 <= n + along < narrow
    ]
    return lax.ppermute(value, ("wide", "narrow"), pairs)


def exchange_geometry(edges):
    face_lo, face_hi, side_lo, side_hi, *corners = edges
    return [
        shift(face_hi, "wide", 1),
        shift(face_lo, "wide", -1),
        shift(side_hi, "narrow", 1),
        shift(side_lo, "narrow", -1),
        *[shift_both(corner, *step) for corner, step in zip(corners, STEPS)],
    ]


def exchange(edges):
    face_lo, face_hi, side_lo, side_hi = edges
    ylo, yhi = shift(side_hi, "narrow", 1), shift(side_lo, "narrow", -1)
    near = jnp.arange(8)[:, None] < 4
    ends = jnp.where(near, yhi[:, :, LX - W :], ylo[:, :, LX - W :])
    face_hi = jnp.concatenate([face_hi, ends], 3)
    ends = jnp.where(near, yhi[:, :, :W], ylo[:, :, :W])
    face_lo = jnp.concatenate([face_lo, ends], 3)
    return [shift(face_hi, "wide", 1), shift(face_lo, "wide", -1), ylo, yhi]


def sections_kernel(first, count, has_prior, visc, coup, *refs):
    v, xlo, xhi, ylo, yhi = refs[:5]
    geo, glo, ghi, gylo, gyhi = refs[5:10]
    gcorners = refs[10:14]
    prior = refs[14] if has_prior else None
    out, vb, a1, gb, rb, sems = refs[14 + has_prior :]
    own_y, low_y, high_y = pl.ds(8, LY), pl.ds(0, 8), pl.ds(8 + LY, 8)
    parts = []
    for part in range(PARTS):
        cells = pl.ds(part * (LX // PARTS), LX // PARTS)
        there = pl.ds(W + part * (LX // PARTS), LX // PARTS)
        parts.append([])
        for source, target, y in (
            (v, vb, own_y),
            (ylo, vb, low_y),
            (yhi, vb, high_y),
            (geo, gb, own_y),
            (gylo, gb, low_y),
            (gyhi, gb, high_y),
        ):
            parts[-1].append((source.at[:, :, cells], target.at[:, :, there, y]))
    for face, part, x in ((xlo, parts[0], pl.ds(0, W)), (xhi, parts[-1], pl.ds(W + LX, W))):
        part.append((face.at[:, :, :, pl.ds(0, LY)], vb.at[:, :, x, own_y]))
        part.append((face.at[:, :, :, pl.ds(LY, 8)], vb.at[:, :, x, low_y]))
        part.append((face.at[:, :, :, pl.ds(LY, 8)], vb.at[:, :, x, high_y]))
    for (up, along), gcorner, layers in zip(STEPS, gcorners, CORNERS):
        y = low_y if along > 0 else high_y
        part = parts[0 if up > 0 else -1]
        for n, (a, d) in enumerate(layers):
            part.append((gcorner.at[n], gb.at[a, :, W - d if up > 0 else W + LX + d - 1, y]))
    for n, (a, d) in enumerate(BELOW):
        parts[0].append((glo.at[n], gb.at[a, :, W - d, own_y]))
    for n, (a, d) in enumerate(ABOVE):
        parts[-1].append((ghi.at[n], gb.at[a, :, W + LX + d - 1, own_y]))
    loads = []
    n = 0
    for part in parts:
        loads.append([])
        for source, target in part:
            loads[-1].append(pltpu.make_async_copy(source, target, sems.at[n]))
            loads[-1][-1].start()
            n += 1
    if has_prior:
        load_prior = pltpu.make_async_copy(prior, rb, sems.at[n])
        load_prior.start()

    def reach(a, b, lane, shift_by, edge):
        a, b = pltpu.roll(a, shift_by, 1), pltpu.roll(b, shift_by, 1)
        if edge:
            return jnp.where(lane, b, a), jnp.where(lane, 0.0, b)
        return jnp.where(lane, 0.0, a), jnp.where(lane, a, b)

    def flow(src, f, x, g, sign, row):
        lanes = lax.broadcasted_iota(jnp.int32, (8, HZ), 1)
        top, bottom = lanes == HZ - 1, lanes == 0
        rows, up_rows, down_rows = pl.ds(row, 8), pl.ds(row + 1, 8), pl.ds(row - 1, 8)
        join = (lambda p, q: p + q) if sign > 0 else (lambda p, q: p - q)
        planes = [[src[f, h, x + n, rows] for h in range(2)] for n in range(-1, STRIP + 1)]
        flux_x = [
            [gb[g, h, x + n - 1, rows] * join(planes[n + 1][h], planes[n][h]) for h in range(2)]
            for n in range(STRIP + 1)
        ]
        totals = []
        for n in range(STRIP):
            here = planes[n + 1]
            above = reach(*here, top, HZ - 1, True)
            flux_z = [gb[g + 2, h, x + n, rows] * join(above[h], here[h]) for h in range(2)]
            below = reach(*flux_z, bottom, 1, False)
            totals.append([])
            for h in range(2):
                c = here[h]
                total = flux_x[n + 1][h] - flux_x[n][h]
                total = total + gb[g + 1, h, x + n, rows] * join(src[f, h, x + n, up_rows], c)
                total = total - gb[g + 1, h, x + n, down_rows] * join(c, src[f, h, x + n, down_rows])
                totals[-1].append(total + (flux_z[h] - below[h]))
        return planes[1:-1], totals

    size = LX // PARTS
    edges = [1] + [1 + part * size for part in range(1, PARTS)] + [PX - 1]
    for part in range(PARTS):
        for copy in loads[part]:
            copy.wait()

        @pl.loop(edges[part], edges[part + 1], step=STRIP)
        def _(x):
            for f in range(count):
                for row in range(4, 12 + LY, 8):
                    c, d = flow(vb, f, x, 0, -1, row)
                    for n in range(STRIP):
                        for h in range(2):
                            at = (h, x + n, pl.ds(row, 8))
                            a1[(f, *at)] = c[n][h] + visc[first + f] * (gb[(6, *at)] * d[n][h])

    @pl.loop(1, PX - 1, step=STRIP)
    def _(x):
        for f in range(count):
            for row in range(4, 12 + LY, 8):
                c, d = flow(a1, f, x, 3, 1, row)
                for n in range(STRIP):
                    for h in range(2):
                        at = (h, x + n, pl.ds(row, 8))
                        vb[(f, *at)] = c[n][h] - gb[(6, *at)] * d[n][h]

    if has_prior:
        load_prior.wait()
    stores = []
    for part in range(PARTS):
        start = part * size

        @pl.loop(start, start + size, step=STRIP)
        def _(x):
            for row in range(0, LY, 8):
                two = []
                own = []
                for f in range(count):
                    c, d = flow(vb, f, x + W, 0, -1, row + 8)
                    two.append(c)
                    own.append(
                        [
                            [
                                c[n][h]
                                + visc[first + f]
                                * (gb[6, h, x + W + n, pl.ds(row + 8, 8)] * d[n][h])
                                for h in range(2)
                            ]
                            for n in range(STRIP)
                        ]
                    )
                for c in range(COMP):
                    for n in range(STRIP):
                        for h in range(2):
                            at = (c, x + n, pl.ds(row, 8), pl.ds(h * HZ, HZ))
                            total = rb[at] if has_prior else None
                            if first <= c < first + count:
                                mine = own[c - first][n][h]
                                total = mine if total is None else total + mine
                            for f in range(count):
                                term = coup[c, first + f] * two[f][n][h]
                                total = term if total is None else total + term
                            rb[at] = total

        cells = pl.ds(start, size)
        stores.append(pltpu.make_async_copy(rb.at[:, cells], out.at[:, cells], sems.at[part]))
        stores[-1].start()
    for store in stores:
        store.wait()


def sections(first, count, visc, coup, v, halos, geo, ghalos, prior):
    operands = [visc, coup, v, *halos, geo, *ghalos]
    if prior is not None:
        operands.append(prior)
    cells = LX * LY * LZ
    return pl.pallas_call(
        functools.partial(sections_kernel, first, count, prior is not None),
        out_shape=struct(COMP, LX, LY, LZ),
        in_specs=[SMEM, SMEM] + [ANY] * (len(operands) - 2),
        out_specs=ANY,
        scratch_shapes=[
            pltpu.VMEM((count, 2, PX, PY, HZ), jnp.float32),
            pltpu.VMEM((count, 2, PX, PY, HZ), jnp.float32),
            pltpu.VMEM((7, 2, PX, PY, HZ), jnp.float32),
            pltpu.VMEM((COMP, LX, LY, LZ), jnp.float32),
            pltpu.SemaphoreType.DMA((100,)),
        ],
        compiler_params=params(),
        cost_estimate=cost(cells * count * 80, 4 * cells * (count + 20)),
        name=f"sections{first}",
    )(*operands)


def on_device(old_fields, old_target, cut_flag, apertures, volume, velocity, diffusivity, coupling):
    wide = lax.axis_size("wide")
    layer = BPY * lax.axis_size("narrow") * BPZ
    blocks = old_fields.shape[0]
    per_peer = blocks // wide
    outgoing = [pack(old_target, old_fields, *chunk, wide, layer) for chunk in CHUNKS]
    received = lax.all_to_all(outgoing[0], "wide", 0, 0, tiled=True)
    geo, edges = geometry(cut_flag, apertures, volume, velocity)
    received, geo, ghalos = lax.optimization_barrier((received, geo, exchange_geometry(edges)))
    slots = received[:, 0, -8, :per_peer].astype(jnp.int32).reshape(blocks)
    ready = []
    for n, (first, count) in enumerate(CHUNKS):
        if n + 1 < len(CHUNKS):
            coming, received = lax.optimization_barrier((outgoing[n + 1], received))
            coming = lax.all_to_all(coming, "wide", 0, 0, tiled=True)
        v, edges = unpack(count, slots, received)
        halos = exchange(edges)
        if n + 1 < len(CHUNKS):
            received, halos = lax.optimization_barrier((coming, halos))
        ready.append((v, halos))
    result = None
    for (first, count), (v, halos) in zip(CHUNKS, ready):
        result = sections(first, count, diffusivity, coupling, v, halos, geo, ghalos, result)
    return result


def solution(mesh):
    in_specs = (
        P(("wide", "narrow"), None, None, None),
        P(("wide", "narrow")),
        P("wide", "narrow", None),
        P(None, "wide", "narrow", None),
        P("wide", "narrow", None),
        P(None, "wide", "narrow", None),
        P(),
        P(),
    )
    out_specs = P(None, "wide", "narrow", None)
    return jax.shard_map(
        on_device, mesh=mesh, in_specs=in_specs, out_specs=out_specs, check_vma=False
    )
```

```python
import functools

import jax
import jax.numpy as jnp
from jax import lax
from jax.experimental import pallas as pl
from jax.experimental.pallas import tpu as pltpu
from jax.sharding import PartitionSpec as P

BE = 16
BPX = 2
BPY = 2
BPZ = 16
COMP = 6
ADVECT = 0.2
W = 3
LX = BPX * BE
LY = BPY * BE
LZ = BPZ * BE
HZ = LZ // 2
PX = LX + 2 * W
PY = LY + 16
CHUNKS = ((0, 4), (4, 2))
ANY = pl.BlockSpec(memory_space=pl.ANY)
SMEM = pl.BlockSpec(memory_space=pltpu.SMEM)
VMEM_LIMIT = 60 * 1024 * 1024
PARTS = 4

BELOW = ((0, 3), (0, 2), (0, 1), (1, 2), (1, 1), (2, 2), (2, 1), (6, 2), (6, 1), (3, 2), (3, 1), (4, 1), (5, 1))
ABOVE = ((0, 1), (0, 2), (1, 1), (1, 2), (2, 1), (2, 2), (6, 1), (6, 2), (3, 1), (4, 1), (5, 1))
CORNERS = (
    ((0, 1), (0, 2), (1, 1), (1, 2), (2, 1), (6, 1), (3, 1), (4, 1)),
    ((0, 1), (0, 2), (1, 1), (2, 1), (6, 1), (3, 1)),
    ((0, 1), (1, 1), (1, 2), (2, 1), (6, 1), (4, 1)),
    ((0, 1), (1, 1), (2, 1), (6, 1)),
)
STEPS = ((1, 1), (1, -1), (-1, 1), (-1, -1))


def struct(*shape):
    return jax.ShapeDtypeStruct(shape, jnp.float32)


def params():
    return pltpu.CompilerParams(vmem_limit_bytes=VMEM_LIMIT)


def cost(flops, moved):
    return pl.CostEstimate(flops=flops, bytes_accessed=moved, transcendentals=0)


def pack_kernel(first, count, wide, layer, tgt, fields, out, buf, header, ids, tally, sem_in, sem_out):
    blocks = tgt.shape[0]
    per_peer = blocks // wide
    rows = per_peer * count * BE

    @pl.loop(0, wide)
    def _(d):
        tally[d] = 0

    @pl.loop(0, blocks)
    def _(b):
        t = tgt[b]
        bx = t // layer
        rest = t - bx * layer
        by = rest // BPZ
        dest = bx // BPX
        rank = tally[dest]
        tally[dest] = rank + 1
        ids[dest * per_peer + rank] = ((bx - dest * BPX) * BPY + by % BPY) * BPZ + rest - by * BPZ
        pltpu.make_async_copy(
            fields.at[b, pl.ds(first, count)], buf.at[dest, rank], sem_in.at[dest]
        ).start()

    if first == 0:
        lane = lax.broadcasted_iota(jnp.int32, (8, HZ), 1)
        for dest in range(wide):
            places = jnp.zeros((8, HZ), jnp.int32)
            for rank in range(per_peer):
                places = jnp.where(lane == rank, ids[dest * per_peer + rank], places)
            header[dest] = places.astype(jnp.float32)
    copies = []
    for dest in range(wide):
        pltpu.make_async_copy(buf.at[dest], buf.at[dest], sem_in.at[dest]).wait()
        merged = buf.at[dest].reshape(rows, LZ)
        pairs = [
            (merged.at[:, pl.ds(half * HZ, HZ)], out.at[dest, half, pl.ds(0, rows)])
            for half in range(2)
        ]
        if first == 0:
            pairs.append((header.at[dest], out.at[dest, 0, pl.ds(rows, 8)]))
            pairs.append((header.at[dest], out.at[dest, 1, pl.ds(rows, 8)]))
        for n, (source, target) in enumerate(pairs):
            copies.append(pltpu.make_async_copy(source, target, sem_out.at[dest, n]))
            copies[-1].start()
    for copy in copies:
        copy.wait()


def pack(old_target, old_fields, first, count, wide, layer):
    blocks = old_fields.shape[0]
    per_peer = blocks // wide
    rows = per_peer * count * BE
    return pl.pallas_call(
        functools.partial(pack_kernel, first, count, wide, layer),
        out_shape=struct(wide, 2, rows + (8 if first == 0 else 0), HZ),
        in_specs=[SMEM, ANY],
        out_specs=ANY,
        scratch_shapes=[
            pltpu.VMEM((wide, per_peer, count, BE, LZ), jnp.float32),
            pltpu.VMEM((wide, 8, HZ), jnp.float32),
            pltpu.SMEM((blocks,), jnp.int32),
            pltpu.SMEM((wide,), jnp.int32),
            pltpu.SemaphoreType.DMA((wide,)),
            pltpu.SemaphoreType.DMA((wide, 4)),
        ],
        compiler_params=params(),
        cost_estimate=cost(0, 8 * wide * rows * LZ),
        name=f"pack{first}",
    )(old_target, old_fields)


def halo_copies(out, v, faces, sides, sems):
    pairs = [
        (out.at[:, :, :, pl.ds(0, 8)], sides[0]),
        (out.at[:, :, :, pl.ds(LY - 8, 8)], sides[1]),
        (out.at[:, :, pl.ds(0, W)], faces[0]),
        (out.at[:, :, pl.ds(LX - W, W)], faces[1]),
        (out, v),
    ]
    return [pltpu.make_async_copy(a, b, sems.at[n]) for n, (a, b) in enumerate(pairs)]


def swap_groups(x):
    row = lax.broadcasted_iota(jnp.int32, x.shape, 0)
    lane = lax.broadcasted_iota(jnp.int32, x.shape, 1)
    skew = (lane + BE * row) % HZ
    turn = (row - lane // BE) % 8
    x = jnp.take_along_axis(x, skew, axis=1, mode="promise_in_bounds")
    x = jnp.take_along_axis(x, turn, axis=0, mode="promise_in_bounds")
    return jnp.take_along_axis(x, skew, axis=1, mode="promise_in_bounds")


def unpack_kernel(counts, ids, *refs):
    arrived = refs[: len(counts)]
    v, face_lo, face_hi, side_lo, side_hi, stage, out, sem_in, sem_out = refs[len(counts) :]
    count = sum(counts)
    unroll = 8 // count
    wide = arrived[0].shape[0]
    per_peer = ids.shape[0] // wide

    @pl.loop(0, wide)
    def _(step):
        for b in range(per_peer):
            slot = ids[step * per_peer + b]
            bz = slot % BPZ
            place = bz // 8 * 8 + (8 - bz % 8) % 8
            begin = 0
            for recv, fields in zip(arrived, counts):
                rows = fields * BE
                pltpu.make_async_copy(
                    recv.at[step, :, pl.ds(b * rows, rows)],
                    stage.at[:, slot // BPZ, pl.ds(begin, rows), place],
                    sem_in.at[slot // BPZ],
                ).start()
                begin += rows

    for q in range(BPX * BPY):
        pltpu.make_async_copy(stage.at[:, q], stage.at[:, q], sem_in.at[q]).wait()

        @pl.loop(0, BE, step=unroll)
        def _(i):
            for j in range(unroll):
                for c in range(count):
                    for half in range(2):
                        for top in range(2):
                            x = stage[half, q, c * BE + i + j, pl.ds(top * 8, 8), :]
                            row = q % BPY * BE + half * 8
                            out[c, top, q // BPY * BE + i + j, pl.ds(row, 8)] = swap_groups(x)

    copies = halo_copies(out, v, (face_lo, face_hi), (side_lo, side_hi), sem_out)
    for copy in copies:
        copy.start()
    for copy in copies:
        copy.wait()


def unpack(counts, ids, arrived):
    count = sum(counts)
    rows = count * BE
    face, side = struct(count, 2, W, LY, HZ), struct(count, 2, LX, 8, HZ)
    v, *edges = pl.pallas_call(
        functools.partial(unpack_kernel, counts),
        out_shape=[struct(count, 2, LX, LY, HZ), face, face, side, side],
        in_specs=[SMEM] + [ANY] * len(counts),
        out_specs=[ANY] * 5,
        scratch_shapes=[
            pltpu.VMEM((2, BPX * BPY, rows, BPZ, HZ), jnp.float32),
            pltpu.VMEM((count, 2, LX, LY, HZ), jnp.float32),
            pltpu.SemaphoreType.DMA((BPX * BPY,)),
            pltpu.SemaphoreType.DMA((5,)),
        ],
        compiler_params=params(),
        cost_estimate=cost(0, 12 * count * LX * LY * LZ),
        name="unpack",
    )(ids, *arrived)
    return v, edges


def geometry_kernel(cut, apertures, volume, velocity, *refs):
    v, low, high, side_lo, side_hi, *corners = refs[:9]
    ap, vo, ve, mask, out, sem_in, sem_out, sem_layer = refs[9:]
    loads = [
        pltpu.make_async_copy(apertures, ap, sem_in.at[0]),
        pltpu.make_async_copy(volume, vo, sem_in.at[1]),
        pltpu.make_async_copy(velocity, ve, sem_in.at[2]),
    ]
    for copy in loads:
        copy.start()
    block_y = lax.broadcasted_iota(jnp.int32, (LY, LZ), 0) // BE
    block_z = lax.broadcasted_iota(jnp.int32, (LY, LZ), 1) // BE
    for bx in range(BPX):
        flags = jnp.zeros((LY, LZ), jnp.int32)
        for by in range(BPY):
            for bz in range(BPZ):
                flags = jnp.where((block_y == by) & (block_z == bz), cut[bx, by, bz], flags)
        mask[bx] = flags
    for copy in loads:
        copy.wait()
    for bx in range(BPX):

        @pl.loop(0, BE)
        def _(i):
            x = bx * BE + i
            for half in range(2):
                z = pl.ds(half * HZ, HZ)
                cut_here = mask[bx, :, z] > 0
                for d in range(3):
                    open_here = jnp.where(cut_here, ap[d, x, :, z], 1.0)
                    out[d, half, x] = open_here
                    out[3 + d, half, x] = open_here * ve[d, x, :, z] * (0.5 * ADVECT)
                out[6, half, x] = 1.0 / jnp.where(cut_here, vo[x, :, z], 1.0)

    copies = [
        pltpu.make_async_copy(out, v, sem_out.at[0]),
        pltpu.make_async_copy(out.at[:, :, :, pl.ds(0, 8)], side_lo, sem_out.at[1]),
        pltpu.make_async_copy(out.at[:, :, :, pl.ds(LY - 8, 8)], side_hi, sem_out.at[2]),
    ]
    n = 0
    for n, (a, d) in enumerate(BELOW):
        copies.append(pltpu.make_async_copy(out.at[a, :, LX - d], low.at[n], sem_layer.at[len(copies)]))
    for n, (a, d) in enumerate(ABOVE):
        copies.append(pltpu.make_async_copy(out.at[a, :, d - 1], high.at[n], sem_layer.at[len(copies)]))
    for (up, along), corner, layers in zip(STEPS, corners, CORNERS):
        y = pl.ds(LY - 8, 8) if along > 0 else pl.ds(0, 8)
        for n, (a, d) in enumerate(layers):
            x = LX - d if up > 0 else d - 1
            copies.append(
                pltpu.make_async_copy(out.at[a, :, x, y], corner.at[n], sem_layer.at[len(copies)])
            )
    for copy in copies:
        copy.start()
    for copy in copies:
        copy.wait()


def geometry(cut_flag, apertures, volume, velocity):
    side = struct(7, 2, LX, 8, HZ)
    low, high = struct(len(BELOW), 2, LY, HZ), struct(len(ABOVE), 2, LY, HZ)
    v, low, high, *rest = pl.pallas_call(
        geometry_kernel,
        out_shape=[struct(7, 2, LX, LY, HZ), low, high, side, side]
        + [struct(len(layers), 2, 8, HZ) for layers in CORNERS],
        in_specs=[SMEM, ANY, ANY, ANY],
        out_specs=[ANY] * 9,
        scratch_shapes=[
            pltpu.VMEM((3, LX, LY, LZ), jnp.float32),
            pltpu.VMEM((LX, LY, LZ), jnp.float32),
            pltpu.VMEM((3, LX, LY, LZ), jnp.float32),
            pltpu.VMEM((BPX, LY, LZ), jnp.int32),
            pltpu.VMEM((7, 2, LX, LY, HZ), jnp.float32),
            pltpu.SemaphoreType.DMA((3,)),
            pltpu.SemaphoreType.DMA((3,)),
            pltpu.SemaphoreType.DMA((64,)),
        ],
        compiler_params=params(),
        cost_estimate=cost(0, 64 * LX * LY * LZ),
        name="geometry",
    )(cut_flag, apertures, volume, velocity)
    return v, [high, low, *rest]


def shift(value, axis, by):
    count = lax.axis_size(axis)
    return lax.ppermute(value, axis, [(i, i + by) for i in range(count) if 0 <= i + by < count])


def shift_both(value, up, along):
    wide, narrow = lax.axis_size("wide"), lax.axis_size("narrow")
    pairs = [
        (w * narrow + n, (w + up) * narrow + n + along)
        for w in range(wide)
        for n in range(narrow)
        if 0 <= w + up < wide and 0 <= n + along < narrow
    ]
    return lax.ppermute(value, ("wide", "narrow"), pairs)


def exchange_geometry(edges):
    face_lo, face_hi, side_lo, side_hi, *corners = edges
    return [
        shift(face_hi, "wide", 1),
        shift(face_lo, "wide", -1),
        shift(side_hi, "narrow", 1),
        shift(side_lo, "narrow", -1),
        *[shift_both(corner, *step) for corner, step in zip(corners, STEPS)],
    ]


def exchange_y(edges):
    face_lo, face_hi, side_lo, side_hi = edges
    ylo, yhi = shift(side_hi, "narrow", 1), shift(side_lo, "narrow", -1)
    near = jnp.arange(8)[:, None] < 4
    ends = jnp.where(near, yhi[:, :, LX - W :], ylo[:, :, LX - W :])
    face_hi = jnp.concatenate([face_hi, ends], 3)
    ends = jnp.where(near, yhi[:, :, :W], ylo[:, :, :W])
    face_lo = jnp.concatenate([face_lo, ends], 3)
    return face_lo, face_hi, ylo, yhi


def exchange_x(face_lo, face_hi, ylo, yhi):
    return [shift(face_hi, "wide", 1), shift(face_lo, "wide", -1), ylo, yhi]


def make_flow(gb):
    def reach(a, b, lane, shift_by, edge):
        a, b = pltpu.roll(a, shift_by, 1), pltpu.roll(b, shift_by, 1)
        if edge:
            return jnp.where(lane, b, a), jnp.where(lane, 0.0, b)
        return jnp.where(lane, 0.0, a), jnp.where(lane, a, b)

    def flow(src, f, x, g, sign, row, strip):
        lanes = lax.broadcasted_iota(jnp.int32, (8, HZ), 1)
        top, bottom = lanes == HZ - 1, lanes == 0
        rows, up_rows, down_rows = pl.ds(row, 8), pl.ds(row + 1, 8), pl.ds(row - 1, 8)
        join = (lambda p, q: p + q) if sign > 0 else (lambda p, q: p - q)
        planes = [[src[f, h, x + n, rows] for h in range(2)] for n in range(-1, strip + 1)]
        flux_x = [
            [gb[g, h, x + n - 1, rows] * join(planes[n + 1][h], planes[n][h]) for h in range(2)]
            for n in range(strip + 1)
        ]
        totals = []
        for n in range(strip):
            here = planes[n + 1]
            above = reach(*here, top, HZ - 1, True)
            flux_z = [gb[g + 2, h, x + n, rows] * join(above[h], here[h]) for h in range(2)]
            below = reach(*flux_z, bottom, 1, False)
            totals.append([])
            for h in range(2):
                c = here[h]
                total = flux_x[n + 1][h] - flux_x[n][h]
                total = total + gb[g + 1, h, x + n, rows] * join(src[f, h, x + n, up_rows], c)
                total = total - gb[g + 1, h, x + n, down_rows] * join(c, src[f, h, x + n, down_rows])
                totals[-1].append(total + (flux_z[h] - below[h]))
        return planes[1:-1], totals

    def diffusive(src, dst, fields, first, x, visc, strip):
        for f in fields:
            for row in range(4, 12 + LY, 8):
                c, d = flow(src, f, x, 0, -1, row, strip)
                for n in range(strip):
                    for h in range(2):
                        at = (h, x + n, pl.ds(row, 8))
                        dst[(f, *at)] = c[n][h] + visc[first + f] * (gb[(6, *at)] * d[n][h])

    def advective(src, dst, fields, x, strip):
        for f in fields:
            for row in range(4, 12 + LY, 8):
                c, d = flow(src, f, x, 3, 1, row, strip)
                for n in range(strip):
                    for h in range(2):
                        at = (h, x + n, pl.ds(row, 8))
                        dst[(f, *at)] = c[n][h] - gb[(6, *at)] * d[n][h]

    def final(src, rb, fields, first, x, into, visc, coup, strip, add):
        for row in range(0, LY, 8):
            two = {}
            own = {}
            for f in fields:
                c, d = flow(src, f, x, 0, -1, row + 8, strip)
                two[f] = c
                own[f] = [
                    [
                        c[n][h] + visc[first + f] * (gb[6, h, x + n, pl.ds(row + 8, 8)] * d[n][h])
                        for h in range(2)
                    ]
                    for n in range(strip)
                ]
            for c in range(COMP):
                for n in range(strip):
                    for h in range(2):
                        at = (c, into + n, pl.ds(row, 8), pl.ds(h * HZ, HZ))
                        total = rb[at] if add else None
                        if c - first in own:
                            mine = own[c - first][n][h]
                            total = mine if total is None else total + mine
                        for f in fields:
                            term = coup[c, first + f] * two[f][n][h]
                            total = term if total is None else total + term
                        rb[at] = total

    return diffusive, advective, final


OWN_Y, LOW_Y, HIGH_Y = pl.ds(8, LY), pl.ds(0, 8), pl.ds(8 + LY, 8)


def middle_kernel(first, count, has_prior, visc, coup, v, ylo, yhi, geo, gylo, gyhi, *refs):
    prior = refs[0] if has_prior else None
    out, vb, a1, gb, rb, sem_in, sem_out = refs[has_prior:]
    size = LX // PARTS
    loads = []
    for part in range(PARTS):
        cells = pl.ds(part * size, size)
        loads.append([])
        for source, target, y in (
            (v, vb, OWN_Y),
            (ylo, vb, LOW_Y),
            (yhi, vb, HIGH_Y),
            (geo, gb, OWN_Y),
            (gylo, gb, LOW_Y),
            (gyhi, gb, HIGH_Y),
        ):
            sem = sem_in.at[part, len(loads[-1])]
            loads[-1].append(
                pltpu.make_async_copy(source.at[:, :, cells], target.at[:, :, cells, y], sem)
            )
            loads[-1][-1].start()
    inner = pl.ds(W, LX - 2 * W)
    if has_prior:
        load_prior = pltpu.make_async_copy(prior.at[:, inner], rb.at[:, inner], sem_in.at[0, 6])
        load_prior.start()
    diffusive, advective, final = make_flow(gb)
    fields = range(count)
    strip = 2 if count < 4 else 1
    edges = [1] + [part * size - 1 for part in range(1, PARTS)] + [LX - 1]
    for part in range(PARTS):
        for copy in loads[part]:
            copy.wait()

        @pl.loop(edges[part], edges[part + 1], step=strip)
        def _(x):
            diffusive(vb, a1, fields, first, x, visc, strip)

    @pl.loop(2, LX - 2, step=strip)
    def _(x):
        advective(a1, vb, fields, x, strip)

    if has_prior:
        load_prior.wait()
    stores = []
    edges = [*range(W, LX - W, size), LX - W]
    for n, (start, stop) in enumerate(zip(edges[:-1], edges[1:])):

        @pl.loop(start, stop, step=2)
        def _(x):
            final(vb, rb, fields, first, x, x, visc, coup, 2, has_prior)

        cells = pl.ds(start, stop - start)
        stores.append(pltpu.make_async_copy(rb.at[:, cells], out.at[:, cells], sem_out.at[n]))
        stores[-1].start()
    for store in stores:
        store.wait()


def middle(first, count, visc, coup, v, ylo, yhi, geo, gylo, gyhi, prior):
    operands = [visc, coup, v, ylo, yhi, geo, gylo, gyhi]
    if prior is not None:
        operands.append(prior)
    cells = LX * LY * LZ
    return pl.pallas_call(
        functools.partial(middle_kernel, first, count, prior is not None),
        out_shape=struct(COMP, LX, LY, LZ),
        in_specs=[SMEM, SMEM] + [ANY] * (len(operands) - 2),
        out_specs=ANY,
        scratch_shapes=[
            pltpu.VMEM((count, 2, LX, PY, HZ), jnp.float32),
            pltpu.VMEM((count, 2, LX, PY, HZ), jnp.float32),
            pltpu.VMEM((7, 2, LX, PY, HZ), jnp.float32),
            pltpu.VMEM((COMP, LX, LY, LZ), jnp.float32),
            pltpu.SemaphoreType.DMA((PARTS, 7)),
            pltpu.SemaphoreType.DMA((8,)),
        ],
        input_output_aliases={} if prior is None else {8: 0},
        compiler_params=params(),
        cost_estimate=cost(cells * count * 60, 4 * cells * (count + 20)),
        name=f"middle{first}",
    )(*operands)


EP = 6 * W


def edges_kernel(counts, visc, coup, *refs):
    groups = [refs[5 * n : 5 * n + 5] for n in range(len(counts))]
    geo, glo, ghi, gylo, gyhi = refs[5 * len(counts) : 5 * len(counts) + 5]
    gcorners = refs[5 * len(counts) + 5 : 5 * len(counts) + 9]
    _, out, vb, a1, gb, rb, sems, sem_out = refs[5 * len(counts) + 9 :]
    ends = ((pl.ds(0, 2 * W), pl.ds(W, 2 * W)), (pl.ds(LX - 2 * W, 2 * W), pl.ds(3 * W, 2 * W)))
    pairs = []
    begin = 0
    for (v, xlo, xhi, ylo, yhi), count in zip(groups, counts):
        of = pl.ds(begin, count)
        begin += count
        for cells, there in ends:
            pairs.append((v.at[:, :, cells], vb.at[of, :, there, OWN_Y]))
            pairs.append((ylo.at[:, :, cells], vb.at[of, :, there, LOW_Y]))
            pairs.append((yhi.at[:, :, cells], vb.at[of, :, there, HIGH_Y]))
        for face, x in ((xlo, pl.ds(0, W)), (xhi, pl.ds(EP - W, W))):
            pairs.append((face.at[:, :, :, pl.ds(0, LY)], vb.at[of, :, x, OWN_Y]))
            pairs.append((face.at[:, :, :, pl.ds(LY, 8)], vb.at[of, :, x, LOW_Y]))
            pairs.append((face.at[:, :, :, pl.ds(LY, 8)], vb.at[of, :, x, HIGH_Y]))
    for cells, there in ends:
        pairs.append((geo.at[:, :, cells], gb.at[:, :, there, OWN_Y]))
        pairs.append((gylo.at[:, :, cells], gb.at[:, :, there, LOW_Y]))
        pairs.append((gyhi.at[:, :, cells], gb.at[:, :, there, HIGH_Y]))
    for (up, along), gcorner, layers in zip(STEPS, gcorners, CORNERS):
        y = LOW_Y if along > 0 else HIGH_Y
        for n, (a, d) in enumerate(layers):
            pairs.append((gcorner.at[n], gb.at[a, :, W - d if up > 0 else EP - W + d - 1, y]))
    for n, (a, d) in enumerate(BELOW):
        pairs.append((glo.at[n], gb.at[a, :, W - d, OWN_Y]))
    for n, (a, d) in enumerate(ABOVE):
        pairs.append((ghi.at[n], gb.at[a, :, EP - W + d - 1, OWN_Y]))
    copies = [pltpu.make_async_copy(a, b, sems.at[n]) for n, (a, b) in enumerate(pairs)]
    for copy in copies:
        copy.start()
    for copy in copies:
        copy.wait()
    diffusive, advective, final = make_flow(gb)
    halves = (range(0, COMP // 2), range(COMP // 2, COMP))
    for fields in halves:
        @pl.loop(1, EP - 1, step=2)
        def _(x):
            diffusive(vb, a1, fields, 0, x, visc, 2)

        @pl.loop(1, EP - 1, step=2)
        def _(x):
            advective(a1, vb, fields, x, 2)

        @pl.loop(0, 2)
        def _(end):
            final(vb, rb, fields, 0, W + end * 3 * W, end * W, visc, coup, W, fields[0] > 0)

    stores = [
        pltpu.make_async_copy(rb.at[:, pl.ds(0, W)], out.at[:, pl.ds(0, W)], sem_out.at[0]),
        pltpu.make_async_copy(rb.at[:, pl.ds(W, W)], out.at[:, pl.ds(LX - W, W)], sem_out.at[1]),
    ]
    for store in stores:
        store.start()
    for store in stores:
        store.wait()


def ends(counts, visc, coup, groups, geo, ghalos, result):
    operands = [visc, coup]
    for group in groups:
        operands += group
    operands += [geo, *ghalos, result]
    cells = LX * LY * LZ
    return pl.pallas_call(
        functools.partial(edges_kernel, counts),
        out_shape=struct(COMP, LX, LY, LZ),
        in_specs=[SMEM, SMEM] + [ANY] * (len(operands) - 2),
        out_specs=ANY,
        scratch_shapes=[
            pltpu.VMEM((COMP, 2, EP, PY, HZ), jnp.float32),
            pltpu.VMEM((COMP, 2, EP, PY, HZ), jnp.float32),
            pltpu.VMEM((7, 2, EP, PY, HZ), jnp.float32),
            pltpu.VMEM((COMP, 2 * W, LY, LZ), jnp.float32),
            pltpu.SemaphoreType.DMA((96,)),
            pltpu.SemaphoreType.DMA((2,)),
        ],
        input_output_aliases={len(operands) - 1: 0},
        compiler_params=params(),
        cost_estimate=cost(cells * 120, 20 * cells),
        name="ends",
    )(*operands)


def on_device(old_fields, old_target, cut_flag, apertures, volume, velocity, diffusivity, coupling):
    wide = lax.axis_size("wide")
    layer = BPY * lax.axis_size("narrow") * BPZ
    blocks = old_fields.shape[0]
    per_peer = blocks // wide
    outgoing = [pack(old_target, old_fields, *chunk, wide, layer) for chunk in CHUNKS]
    received = lax.all_to_all(outgoing[0], "wide", 0, 0, tiled=True)
    geo, edges = geometry(cut_flag, apertures, volume, velocity)
    glo, ghi, gylo, gyhi, *gcorners = exchange_geometry(edges)
    received, geo, gylo, gyhi = lax.optimization_barrier((received, geo, gylo, gyhi))
    ghalos = [glo, ghi, gylo, gyhi, *gcorners]
    slots = received[:, 0, -8, :per_peer].astype(jnp.int32).reshape(blocks)
    groups = []
    result = None
    for n, (first, count) in enumerate(CHUNKS):
        if n + 1 < len(CHUNKS):
            coming, received = lax.optimization_barrier((outgoing[n + 1], received))
            coming = lax.all_to_all(coming, "wide", 0, 0, tiled=True)
        v, edges = unpack((count,), slots, [received])
        xlo, xhi, ylo, yhi = exchange_x(*exchange_y(edges))
        result = middle(
            first, count, diffusivity, coupling, v, ylo, yhi, geo, gylo, gyhi, result
        )
        if n + 1 < len(CHUNKS):
            received, result, ghalos = lax.optimization_barrier((coming, result, ghalos))
        groups.append((v, xlo, xhi, ylo, yhi))
    counts = tuple(count for _, count in CHUNKS)
    return ends(counts, diffusivity, coupling, groups, geo, ghalos, result)


def solution(mesh):
    in_specs = (
        P(("wide", "narrow"), None, None, None),
        P(("wide", "narrow")),
        P("wide", "narrow", None),
        P(None, "wide", "narrow", None),
        P("wide", "narrow", None),
        P(None, "wide", "narrow", None),
        P(),
        P(),
    )
    out_specs = P(None, "wide", "narrow", None)
    return jax.shard_map(
        on_device, mesh=mesh, in_specs=in_specs, out_specs=out_specs, check_vma=False
    )
```
